32 devices in a mesh: fsdp: 8 (over z, x), ctx: 4 (over y, core).
Axes of the slice: x: 2, y: 2, z: 4, core: 2. Of those that a mesh axis runs over, the one named last changes fastest.
Arguments:
- tokens: bfloat16 [8, 512, 960], P('fsdp', 'ctx'), may hold values from -6 to 6
- gain_attn: bfloat16 [960], P('fsdp'), may hold values from 0.5 to 1.5
- w_qkv: bfloat16 [960, 1600], P('fsdp'), may hold values from -1 to 1
- w_out: bfloat16 [960, 960], P('fsdp'), may hold values from -0.5 to 0.5
- gain_ffn: bfloat16 [960], P('fsdp'), may hold values from 0.5 to 1.5
- w_gate_up: bfloat16 [2, 960, 2560], P(None, 'fsdp'), may hold values from -0.1875 to 0.1875
- w_down: bfloat16 [2560, 960], P('fsdp'), may hold values from -0.125 to 0.125
- cotangent: bfloat16 [8, 512, 960], P('fsdp', 'ctx'), may hold values from -6 to 6
Outputs:
- block_out: bfloat16 [8, 512, 960], P('fsdp', 'ctx')
- input_grad: float32 [8, 512, 960], P('fsdp', 'ctx')
- grad_gain_attn: float32 [960], P('fsdp')
- grad_qkv: float32 [960, 1600], P('fsdp')
- grad_out: float32 [960, 960], P('fsdp')
- grad_gain_ffn: float32 [960], P('fsdp')
- grad_gate_up: float32 [2, 960, 2560], P(None, 'fsdp')
- grad_down: float32 [2560, 960], P('fsdp')
The draws below stay inside these ranges and needn't reach their ends.
All inputs are finite; a program needn't handle non-finite values.
Results may differ from the reference program's by a relative error of at most 0.03.
Values may be sent and summed in bfloat16 or wider, within the bound.
No kernel may reach another device: no remote copies, remote signals or barrier semaphores. Data moves between devices by JAX's collectives and lax.ppermute only.
A program may use at most 192 MiB of HBM per device.

```python
import jax
import jax.numpy as jnp
from jax import lax

D = 960
H = 15
KVH = 5
HD = 64
FF = 2560
LEN = 512
SEQS = 8
QKV = 1600


def draw_tokens(key, part):
    base_key = jax.random.fold_in(key, 11)
    values = jax.random.truncated_normal(base_key, -6.0, 6.0, (SEQS, LEN, D), jnp.float32)
    return values.astype(jnp.bfloat16)


def draw_w_qkv(key, part):
    base_key = jax.random.fold_in(key, 21)
    values = jax.random.truncated_normal(base_key, -6.0, 6.0, (D, QKV), jnp.float32) * D ** (-0.5)
    return values.astype(jnp.bfloat16)


def shard_levels(stream_key, extent, pieces, smallest, top_value):
    level = 1.0
    for axis_at, blocks in pieces:
        steps = jax.random.uniform(jax.random.fold_in(jax.random.fold_in(stream_key, 6), axis_at), (blocks,), jnp.float32, smallest / len(pieces), top_value / len(pieces))
        level = level * jnp.repeat(jnp.exp(steps), extent[axis_at] // blocks).reshape((-1,) + (1,) * (len(extent) - 1 - axis_at))
    return level


def normal_values(rng, shape, spread, most, pieces=(), kind=jnp.bfloat16):
    entries = spread * jax.random.normal(rng, shape, jnp.float32)
    if pieces:
        entries = entries * shard_levels(rng, shape, pieces, -0.22, 0.18)
    return jnp.clip(entries, -most, most).astype(kind)


def setup_inputs(seed: int = 0) -> dict:
    arg_keys = jax.random.split(jax.random.key(seed), 9)
    tokens = draw_tokens(jax.random.fold_in(arg_keys[8], 71), 0)
    gain_attn = jnp.clip(1.0 + 0.1 * jax.random.normal(arg_keys[1], (D,), jnp.float32), 0.5, 1.5).astype(jnp.bfloat16)
    w_qkv = draw_w_qkv(jax.random.fold_in(arg_keys[8], 71), 0)
    w_out = normal_values(arg_keys[3], (H * HD, D), (D // 8) ** -0.5, 0.5, ((0, 8),))
    gain_ffn = jnp.clip(1.0 + 0.1 * jax.random.normal(arg_keys[4], (D,), jnp.float32), 0.5, 1.5).astype(jnp.bfloat16)
    w_gate_up = normal_values(arg_keys[5], (2, D, FF), D ** -0.5, 0.1875, ((1, 8),))
    w_down = normal_values(arg_keys[6], (FF, D), FF ** -0.5, 0.125, ((0, 8),))
    cotangent = normal_values(arg_keys[7], (SEQS, LEN, D), 1.0, 6.0, ((0, 8), (1, 4)))
    return {"tokens": tokens, "gain_attn": gain_attn, "w_qkv": w_qkv, "w_out": w_out, "gain_ffn": gain_ffn, "w_gate_up": w_gate_up, "w_down": w_down, "cotangent": cotangent}


EPS = 1e-05

def rounded(values):
    return lax.optimization_barrier(values.astype(jnp.bfloat16)).astype(jnp.float32)

def rope_tables(length, offset):
    half = HD // 2
    position = (offset + jnp.arange(length)).astype(jnp.float32)
    freqs = jnp.exp(-jnp.log(10000.0) * jnp.arange(half).astype(jnp.float32) / half)
    angles = position[:, None] * freqs[None, :]
    return (jnp.cos(angles), jnp.sin(angles))

def rotate(values, cosine, sine):
    half = values.shape[-1] // 2
    lower = values[..., :half]
    upper = values[..., half:]
    cos_part = cosine[:, None, :]
    sin_part = sine[:, None, :]
    return jnp.concatenate([lower * cos_part - upper * sin_part, upper * cos_part + lower * sin_part], -1)

def rotate_back(values, cosine, sine):
    half = values.shape[-1] // 2
    lower = values[..., :half]
    upper = values[..., half:]
    cos_part = cosine[:, None, :]
    sin_part = sine[:, None, :]
    return jnp.concatenate([lower * cos_part + upper * sin_part, upper * cos_part - lower * sin_part], -1)

def one_sequence(inputs, cots, weights):
    gain_one, w_qkv, w_out, gain_two, w_gate_up, w_down = weights
    length = inputs.shape[0]
    groups = H // KVH
    scale = HD ** (-0.5)
    xfloat = inputs.astype(jnp.float32)
    r_one = lax.rsqrt(lax.optimization_barrier(jnp.mean(xfloat * xfloat, -1, keepdims=True)) + EPS)
    z_one = xfloat * r_one
    g_one = gain_one.astype(jnp.float32)
    h_one = (z_one * g_one).astype(jnp.bfloat16)
    qkv = jnp.dot(h_one, w_qkv, preferred_element_type=jnp.float32)
    cosine, sine = rope_tables(length, 0)
    query = rotate(qkv[:, :H * HD].reshape(length, H, HD), cosine, sine).astype(jnp.bfloat16)
    keys = rotate(qkv[:, H * HD:(H + KVH) * HD].reshape(length, KVH, HD), cosine, sine).astype(jnp.bfloat16)
    values = qkv[:, (H + KVH) * HD:].reshape(length, KVH, HD).astype(jnp.bfloat16)
    q_group = query.reshape(length, KVH, groups, HD).astype(jnp.float32)
    k_float = keys.astype(jnp.float32)
    v_float = values.astype(jnp.float32)
    scores = jnp.einsum('igrd,jgd->grij', q_group, k_float) * scale
    rows = jnp.arange(length)
    allowed = rows[:, None] >= rows[None, :]
    scores = jnp.where(allowed, scores, -1e+30)
    top_score = lax.optimization_barrier(jnp.max(scores, -1))
    weights_soft = jnp.where(allowed, jnp.exp(scores - top_score[..., None]), 0.0)
    total = lax.optimization_barrier(jnp.sum(weights_soft, -1))
    log_total = top_score + jnp.log(total)
    mixed = jnp.einsum('grij,jgd->grid', rounded(weights_soft), v_float) / total[..., None]
    attn_out = mixed.transpose(2, 0, 1, 3).reshape(length, H * HD).astype(jnp.bfloat16)
    resid = xfloat + jnp.dot(attn_out, w_out, preferred_element_type=jnp.float32)
    r_two = lax.rsqrt(lax.optimization_barrier(jnp.mean(resid * resid, -1, keepdims=True)) + EPS)
    z_two = resid * r_two
    g_two = gain_two.astype(jnp.float32)
    h_two = (z_two * g_two).astype(jnp.bfloat16)
    gate = jnp.dot(h_two, w_gate_up[0], preferred_element_type=jnp.float32)
    upper = jnp.dot(h_two, w_gate_up[1], preferred_element_type=jnp.float32)
    sigma = jax.nn.sigmoid(gate)
    gated = (gate * sigma * upper).astype(jnp.bfloat16)
    result = (resid + jnp.dot(gated, w_down, preferred_element_type=jnp.float32)).astype(jnp.bfloat16)
    cfloat = cots.astype(jnp.float32)
    grad_down = jnp.dot(gated.T, cots, preferred_element_type=jnp.float32)
    d_gated = jnp.dot(cots, w_down.T, preferred_element_type=jnp.float32)
    d_gate = (d_gated * upper * sigma * (1.0 + gate * (1.0 - sigma))).astype(jnp.bfloat16)
    d_upper = (d_gated * gate * sigma).astype(jnp.bfloat16)
    grad_gate_up = jnp.stack([jnp.dot(h_two.T, d_gate, preferred_element_type=jnp.float32), jnp.dot(h_two.T, d_upper, preferred_element_type=jnp.float32)])
    d_h_two = jnp.dot(d_gate, w_gate_up[0].T, preferred_element_type=jnp.float32) + jnp.dot(d_upper, w_gate_up[1].T, preferred_element_type=jnp.float32)
    grad_gain_two = lax.optimization_barrier(jnp.sum(d_h_two * z_two, 0))
    d_z_two = d_h_two * g_two
    d_resid = cfloat + r_two * (d_z_two - z_two * lax.optimization_barrier(jnp.mean(d_z_two * z_two, -1, keepdims=True)))
    d_resid_b = d_resid.astype(jnp.bfloat16)
    grad_out = jnp.dot(attn_out.T, d_resid_b, preferred_element_type=jnp.float32)
    d_attn = jnp.dot(d_resid_b, w_out.T, preferred_element_type=jnp.float32).astype(jnp.bfloat16)
    d_group = d_attn.reshape(length, KVH, groups, HD).transpose(1, 2, 0, 3).astype(jnp.float32)
    o_group = attn_out.reshape(length, KVH, groups, HD).transpose(1, 2, 0, 3).astype(jnp.float32)
    delta = lax.optimization_barrier(jnp.sum(d_group * o_group, -1))
    probs = jnp.where(allowed, jnp.exp(scores - log_total[..., None]), 0.0)
    d_values = jnp.einsum('grij,grid->jgd', rounded(probs), d_group)
    d_probs = jnp.einsum('grid,jgd->grij', d_group, v_float)
    d_scores = rounded(probs * (d_probs - delta[..., None]))
    d_query = scale * jnp.einsum('grij,jgd->igrd', d_scores, k_float).reshape(length, H, HD)
    d_keys = scale * jnp.einsum('grij,igrd->jgd', d_scores, q_group)
    d_query = rotate_back(d_query, cosine, sine)
    d_keys = rotate_back(d_keys, cosine, sine)
    d_qkv = jnp.concatenate([d_query.reshape(length, H * HD), d_keys.reshape(length, KVH * HD), d_values.reshape(length, KVH * HD)], 1).astype(jnp.bfloat16)
    grad_qkv = jnp.dot(h_one.T, d_qkv, preferred_element_type=jnp.float32)
    d_h_one = jnp.dot(d_qkv, w_qkv.T, preferred_element_type=jnp.float32)
    grad_gain_one = lax.optimization_barrier(jnp.sum(d_h_one * z_one, 0))
    d_z_one = d_h_one * g_one
    d_input = d_resid + r_one * (d_z_one - z_one * lax.optimization_barrier(jnp.mean(d_z_one * z_one, -1, keepdims=True)))
    return (result, d_input, (grad_gain_one, grad_qkv, grad_out, grad_gain_two, grad_gate_up, grad_down))

def reference(tokens, gain_attn, w_qkv, w_out, gain_ffn, w_gate_up, w_down, cotangent):
    weights = (gain_attn, w_qkv, w_out, gain_ffn, w_gate_up, w_down)
    zeros = jax.tree.map(lambda weight: jnp.zeros(weight.shape, jnp.float32), weights)

    def visit(carry, pair):
        result, d_input, grads = one_sequence(pair[0], pair[1], weights)
        return (jax.tree.map(lambda left, right: left + right, carry, grads), (result, d_input))
    totals, (results, d_inputs) = lax.scan(visit, zeros, (tokens, cotangent))
    return (results, d_inputs, totals[0], totals[1], totals[2], totals[3], totals[4], totals[5])
```

```python
import jax
import jax.numpy as jnp
from jax import lax
from jax.sharding import PartitionSpec as P

H = 15
KVH = 5
HD = 64
EPS = 1e-05
F32 = jnp.float32
BF16 = jnp.bfloat16


def mm(left, right, dims=((1,), (0,))):
    return lax.dot_general(left, right, (dims, ((), ())), preferred_element_type=F32)


def swap(value, axis, flip):
    size = lax.axis_size(axis)
    return lax.ppermute(value, axis, [(i, i ^ flip) for i in range(size)])


def pick(stack, index):
    return lax.dynamic_index_in_dim(stack, index, 0, keepdims=False)


def high_bits(size):
    bits = []
    bit = size // 2
    while bit:
        bits.append(bit)
        bit //= 2
    return bits


def ctx_gather(value):
    rank = lax.axis_index("ctx")
    buf = value[None]
    for bit in high_bits(lax.axis_size("ctx")):
        other = swap(buf, "ctx", bit)
        first = (rank & bit) == 0
        low = jnp.where(first, buf, other)
        high = jnp.where(first, other, buf)
        buf = jnp.stack([low, high], 1).reshape((-1,) + value.shape)
    return buf


def ctx_sum_scatter(parts):
    rank = lax.axis_index("ctx")
    buf = parts
    for bit in reversed(high_bits(lax.axis_size("ctx"))):
        pairs = buf.reshape((-1, 2) + buf.shape[1:])
        first = (rank & bit) == 0
        keep = jnp.where(first, pairs[:, 0], pairs[:, 1])
        send = jnp.where(first, pairs[:, 1], pairs[:, 0])
        buf = keep.astype(F32) + swap(send.astype(BF16), "ctx", bit).astype(F32)
    return buf[0]


def ctx_exchange(blocks):
    rank = lax.axis_index("ctx")
    out = blocks
    for k in range(1, lax.axis_size("ctx")):
        got = swap(pick(blocks, rank ^ k), "ctx", k)
        out = lax.dynamic_update_index_in_dim(out, got, rank ^ k, 0)
    return out


def fsdp_gather(value, dim=0):
    size = lax.axis_size("fsdp")
    me = lax.axis_index("fsdp")
    pieces = {}
    for k in range(0, size, 2):
        pieces[k] = value if k == 0 else swap(value, "fsdp", k)
    for k in range(0, size, 2):
        pieces[k + 1] = swap(pieces[k], "fsdp", 1)
    shape = value.shape[:dim] + (size,) + value.shape[dim:]
    out = jnp.zeros(shape, value.dtype)
    for k in range(size):
        out = lax.dynamic_update_index_in_dim(out, pieces[k], me ^ k, dim)
    return out


def fsdp_sum_scatter(parts, dim=0, kind=BF16):
    size = lax.axis_size("fsdp")
    me = lax.axis_index("fsdp")

    def block(index):
        return lax.dynamic_index_in_dim(parts, index, dim, keepdims=False)

    total = None
    for k in reversed(range(0, size, 2)):
        sent = swap(block(me ^ k ^ 1).astype(kind), "fsdp", 1)
        pair = block(me ^ k).astype(F32) + sent.astype(F32)
        if k:
            pair = swap(pair.astype(kind), "fsdp", k).astype(F32)
        total = pair if total is None else total + pair
    return total


def rope_tables(length):
    half = HD // 2
    position = jnp.arange(length, dtype=jnp.int32).astype(F32)
    freqs = jnp.exp(-jnp.log(10000.0) * jnp.arange(half).astype(F32) / half)
    angles = position[:, None] * freqs[None, :]
    return (jnp.cos(angles), jnp.sin(angles))


def rotate(values, cosine, sine):
    half = values.shape[-1] // 2
    lower = values[..., :half]
    upper = values[..., half:]
    cos_part = cosine[:, None, :]
    sin_part = sine[:, None, :]
    return jnp.concatenate(
        [lower * cos_part - upper * sin_part, upper * cos_part + lower * sin_part], -1
    )


def body(tokens, gain_attn, w_qkv, w_out, gain_ffn, w_gate_up, w_down, cotangent):
    ranks = lax.axis_size("ctx")
    owners = lax.axis_size("fsdp")
    rank = lax.axis_index("ctx")
    x_loc = tokens[0]
    cot_loc = cotangent[0]
    length, width = x_loc.shape
    total_len = length * ranks
    rows = w_qkv.shape[0]
    groups = H // KVH
    scale = HD ** (-0.5)
    mine = -(-H // ranks)
    kv_first = [(r * mine) // groups for r in range(ranks)]
    kv_mine = max((r * mine + mine - 1) // groups - kv_first[r] + 1 for r in range(ranks))
    kv_pad = max(kv_first) + kv_mine
    kv_base = (rank * mine) // groups
    hidden = w_down.shape[0] * owners
    part_rows = w_down.shape[0] // ranks
    part = hidden // ranks
    out_cols = w_out.shape[1] // ranks

    q_pad = jnp.pad(w_qkv[:, : H * HD], ((0, 0), (0, (ranks * mine - H) * HD)))
    k_pad = jnp.pad(w_qkv[:, H * HD : (H + KVH) * HD], ((0, 0), (0, (kv_pad - KVH) * HD)))
    v_pad = jnp.pad(w_qkv[:, (H + KVH) * HD :], ((0, 0), (0, (kv_pad - KVH) * HD)))
    qkv_part = jnp.concatenate(
        [
            lax.dynamic_slice_in_dim(q_pad, rank * mine * HD, mine * HD, 1),
            lax.dynamic_slice_in_dim(k_pad, kv_base * HD, kv_mine * HD, 1),
            lax.dynamic_slice_in_dim(v_pad, kv_base * HD, kv_mine * HD, 1),
        ],
        1,
    )
    out_part = lax.dynamic_slice_in_dim(w_out, rank * out_cols, out_cols, 1)
    column = jnp.arange(part, dtype=jnp.int32)
    source = (column // part_rows) * w_down.shape[0] + rank * part_rows + column % part_rows
    chooser = (jnp.arange(hidden, dtype=jnp.int32)[:, None] == source[None, :]).astype(BF16)
    gu_part = mm(w_gate_up.reshape(2 * rows, hidden), chooser).astype(BF16).reshape(2, rows, part)
    down_part = lax.dynamic_slice_in_dim(w_down, rank * part_rows, part_rows, 0)

    gains = fsdp_gather(jnp.stack([gain_attn, gain_ffn]), 1).reshape(2, width).astype(F32)
    g_one = gains[0]
    g_two = gains[1]
    x_all = ctx_gather(x_loc).reshape(total_len, width)
    qkv_full = fsdp_gather(qkv_part).reshape(width, -1)
    cot_all = ctx_gather(cot_loc).reshape(total_len, width)
    out_cols_full = fsdp_gather(out_part).reshape(H * HD, out_cols)
    out_full = ctx_gather(out_cols_full).transpose(1, 0, 2).reshape(H * HD, width)
    gu_full = fsdp_gather(gu_part, 1).reshape(2, width, part)
    down_full = fsdp_gather(down_part).reshape(part, width)

    x_float = x_all.astype(F32)
    r_all = lax.rsqrt(jnp.mean(x_float * x_float, -1, keepdims=True) + EPS)
    z_all = x_float * r_all
    h_all = (z_all * g_one).astype(BF16)
    qkv = mm(h_all, qkv_full)
    cosine, sine = rope_tables(total_len)
    n_q = mine * HD
    n_kv = kv_mine * HD
    query = rotate(qkv[:, :n_q].reshape(total_len, mine, HD), cosine, sine).astype(BF16)
    keys = rotate(qkv[:, n_q : n_q + n_kv].reshape(total_len, kv_mine, HD), cosine, sine).astype(
        BF16
    )
    values = qkv[:, n_q + n_kv :].reshape(total_len, kv_mine, HD).astype(BF16)
    q_heads = query.transpose(1, 0, 2)
    k_all = keys.transpose(1, 0, 2)
    v_all = values.transpose(1, 0, 2)
    which = [(rank * mine + j) // groups - kv_base for j in range(mine)]
    k_heads = jnp.stack([pick(k_all, w) for w in which])
    v_heads = jnp.stack([pick(v_all, w) for w in which])
    batch = ((0,), (0,))
    scores = lax.dot_general(
        q_heads, k_heads, (((2,), (2,)), batch), preferred_element_type=F32
    ) * scale
    at = jnp.arange(total_len, dtype=jnp.int32)
    allowed = at[:, None] >= at[None, :]
    scores = jnp.where(allowed, scores, -1e30)
    top = jnp.max(scores, -1, keepdims=True)
    probs = jnp.where(allowed, jnp.exp(scores - top), 0.0)
    row_sum = jnp.sum(probs, -1, keepdims=True)
    weighted = lax.dot_general(
        probs.astype(BF16), v_heads, (((2,), (1,)), batch), preferred_element_type=F32
    )
    log_total = top + jnp.log(row_sum)
    o_heads = (weighted / row_sum).astype(BF16)
    mixed = o_heads.transpose(1, 0, 2).reshape(ranks, length, n_q)
    attn_loc = ctx_exchange(mixed).transpose(1, 0, 2).reshape(length, ranks * n_q)[:, : H * HD]

    xl = x_loc.astype(F32)
    resid = xl + mm(attn_loc, out_full)
    r_two = lax.rsqrt(jnp.mean(resid * resid, -1, keepdims=True) + EPS)
    z_two = resid * r_two
    h_two = ctx_gather((z_two * g_two).astype(BF16)).reshape(total_len, width)
    gate = mm(h_two, gu_full[0])
    upper = mm(h_two, gu_full[1])
    sigma = jax.nn.sigmoid(gate)
    gated = (gate * sigma * upper).astype(BF16)
    d_gated = mm(cot_all, down_full, ((1,), (1,)))
    d_gate = (d_gated * upper * sigma * (1.0 + gate * (1.0 - sigma))).astype(BF16)
    d_upper = (d_gated * gate * sigma).astype(BF16)
    d_h_part = mm(d_gate, gu_full[0], ((1,), (1,))) + mm(d_upper, gu_full[1], ((1,), (1,)))
    d_h_two = ctx_sum_scatter(d_h_part.reshape(ranks, length, width))
    down_sum = ctx_sum_scatter(mm(gated, down_full).reshape(ranks, length, width))
    result = (resid + down_sum).astype(BF16)
    cfloat = cot_loc.astype(F32)
    grad_gain_two = jnp.sum(d_h_two * z_two, 0)
    d_z_two = d_h_two * g_two
    d_resid = cfloat + r_two * (d_z_two - z_two * jnp.mean(d_z_two * z_two, -1, keepdims=True))
    d_resid_b = d_resid.astype(BF16)

    d_attn_loc = mm(d_resid_b, out_full, ((1,), (1,))).astype(BF16)
    d_blocks = jnp.pad(d_attn_loc, ((0, 0), (0, ranks * n_q - H * HD)))
    d_blocks = d_blocks.reshape(length, ranks, n_q).transpose(1, 0, 2)
    d_mixed = ctx_exchange(d_blocks).reshape(total_len, mine, HD)
    d_heads = d_mixed.transpose(1, 0, 2)
    delta = jnp.sum(d_heads.astype(F32) * o_heads.astype(F32), -1, keepdims=True)
    probs_b = jnp.where(allowed, jnp.exp(scores - log_total), 0.0)
    d_v = lax.dot_general(
        probs_b.astype(BF16), d_heads, (((1,), (1,)), batch), preferred_element_type=F32
    )
    d_probs = lax.dot_general(d_heads, v_heads, (((2,), (2,)), batch), preferred_element_type=F32)
    d_scores = (probs_b * (d_probs - delta)).astype(BF16)
    d_q = scale * lax.dot_general(
        d_scores, k_heads, (((2,), (1,)), batch), preferred_element_type=F32
    )
    d_k = scale * lax.dot_general(
        d_scores, q_heads, (((1,), (1,)), batch), preferred_element_type=F32
    )
    d_k_own = jnp.stack(
        [sum(jnp.where(which[j] == s, d_k[j], 0.0) for j in range(mine)) for s in range(kv_mine)]
    )
    d_v_own = jnp.stack(
        [sum(jnp.where(which[j] == s, d_v[j], 0.0) for j in range(mine)) for s in range(kv_mine)]
    )
    d_q = rotate(d_q.transpose(1, 0, 2), cosine, -sine)
    d_k_own = rotate(d_k_own.transpose(1, 0, 2), cosine, -sine)
    d_qkv = jnp.concatenate(
        [
            d_q.reshape(total_len, n_q),
            d_k_own.reshape(total_len, n_kv),
            d_v_own.transpose(1, 0, 2).reshape(total_len, n_kv),
        ],
        1,
    ).astype(BF16)
    d_one_part = mm(d_qkv, qkv_full, ((1,), (1,)))
    d_h_one = ctx_sum_scatter(d_one_part.reshape(ranks, length, width))
    grad_gain_one = jnp.sum(d_one_part * z_all, 0)
    r_one = lax.rsqrt(jnp.mean(xl * xl, -1, keepdims=True) + EPS)
    z_one = xl * r_one
    d_z_one = d_h_one * g_one
    d_input = d_resid + r_one * (d_z_one - z_one * jnp.mean(d_z_one * z_one, -1, keepdims=True))

    t_dims = ((0,), (0,))
    grad_gu = jnp.stack([mm(h_two, d_gate, t_dims), mm(h_two, d_upper, t_dims)])
    gu_own = fsdp_sum_scatter(grad_gu.reshape(2, owners, rows, part), 1).astype(BF16)
    gu_all = ctx_gather(gu_own)
    gu_out = (
        gu_all.reshape(ranks, 2, rows, owners, part_rows)
        .transpose(1, 2, 3, 0, 4)
        .reshape(2, rows, hidden)
        .astype(F32)
    )
    grad_down = mm(gated, cot_all, t_dims).reshape(owners, part_rows, width)
    down_out = ctx_gather(fsdp_sum_scatter(grad_down).astype(BF16)).reshape(-1, width).astype(F32)
    grad_out = mm(attn_loc, d_resid_b, t_dims).reshape(H * HD, ranks, out_cols).transpose(1, 0, 2)
    grad_out = ctx_sum_scatter(grad_out).reshape(owners, -1, out_cols)
    out_own = fsdp_sum_scatter(grad_out).astype(BF16)
    out_out = ctx_gather(out_own).transpose(1, 0, 2).reshape(-1, width).astype(F32)
    grad_qkv = mm(h_all, d_qkv, t_dims).reshape(owners, rows, -1)
    qkv_own = ctx_gather(fsdp_sum_scatter(grad_qkv).astype(BF16)).astype(F32)
    q_out = qkv_own[:, :, :n_q].transpose(1, 0, 2).reshape(rows, ranks * n_q)[:, : H * HD]
    kv_out = []
    for start in (n_q, n_q + n_kv):
        for head in range(KVH):
            terms = [
                qkv_own[r, :, start + s * HD : start + (s + 1) * HD]
                for r in range(ranks)
                for s in range(kv_mine)
                if kv_first[r] + s == head
            ]
            kv_out.append(sum(terms))
    qkv_out = jnp.concatenate([q_out] + kv_out, 1)
    both_gains = jnp.stack([grad_gain_one, grad_gain_two])
    for bit in high_bits(ranks):
        both_gains = both_gains + swap(both_gains, "ctx", bit)
    gains_out = fsdp_sum_scatter(both_gains.reshape(2, owners, rows), 1, F32)
    return (
        result[None],
        d_input[None],
        gains_out[0],
        qkv_out,
        out_out,
        gains_out[1],
        gu_out,
        down_out,
    )


def solution(mesh):
    in_specs = (
        P("fsdp", "ctx", None),
        P("fsdp"),
        P("fsdp", None),
        P("fsdp", None),
        P("fsdp"),
        P(None, "fsdp", None),
        P("fsdp", None),
        P("fsdp", "ctx", None),
    )
    out_specs = (
        P("fsdp", "ctx", None),
        P("fsdp", "ctx", None),
        P("fsdp"),
        P("fsdp", None),
        P("fsdp", None),
        P("fsdp"),
        P(None, "fsdp", None),
        P("fsdp", None),
    )
    return jax.shard_map(body, mesh=mesh, in_specs=in_specs, out_specs=out_specs, check_vma=False)
```

```python
import jax
import jax.numpy as jnp
from jax import lax
from jax.experimental import pallas as pl
from jax.experimental.pallas import tpu as pltpu
from jax.sharding import PartitionSpec as P

H = 15
KVH = 5
HD = 64
EPS = 1e-05
F32 = jnp.float32
BF16 = jnp.bfloat16
LANES = 128
ROWS = (((0,), (0,)), ((), ()))
COLS = (((1,), (1,)), ((), ()))
PLAIN = (((1,), (0,)), ((), ()))


def dot(left, right, dims=PLAIN):
    return lax.dot_general(left, right, dims, preferred_element_type=F32)


def up_to(value, step):
    return -(-value // step) * step


def shape(dims, kind):
    return jax.ShapeDtypeStruct(dims, kind)


def swap(value, axis, flip):
    size = lax.axis_size(axis)
    return lax.ppermute(value, axis, [(i, i ^ flip) for i in range(size)])


def run(kernel, name, outs, ids, args, scratch=()):
    vmem = pl.BlockSpec(memory_space=pltpu.VMEM)
    return pl.pallas_call(
        kernel,
        name=name,
        out_shape=outs,
        in_specs=[pl.BlockSpec(memory_space=pltpu.SMEM)] + [vmem] * len(args),
        out_specs=jax.tree.map(lambda _: vmem, outs),
        scratch_shapes=[pltpu.VMEM(dims, kind) for dims, kind in scratch],
    )(ids, *args)


class Plan:
    def __init__(self, tokens, w_qkv, w_down):
        self.ranks = lax.axis_size("ctx")
        self.owners = lax.axis_size("fsdp")
        self.length, self.width = tokens.shape[1:]
        self.total = self.length * self.ranks
        self.rows = w_qkv.shape[0]
        self.group = H // KVH
        self.heads = -(-H // self.ranks)
        self.kv_first = [(r * self.heads) // self.group for r in range(self.ranks)]
        self.kv = max(
            (r * self.heads + self.heads - 1) // self.group - self.kv_first[r] + 1
            for r in range(self.ranks)
        )
        self.kv_pad = max(self.kv_first) + self.kv
        self.q_cols = self.heads * HD
        self.kv_cols = self.kv * HD
        self.used = self.q_cols + 2 * self.kv_cols
        self.qkv_cols = up_to(self.used, LANES)
        self.out_cols = self.width // self.ranks
        self.out_pad = up_to(self.out_cols, LANES)
        self.pack_rows = up_to(self.rows + 2, 16)
        self.pack_cols = self.qkv_cols + self.out_pad
        self.part_rows = w_down.shape[0] // self.ranks
        self.hidden = w_down.shape[0] * self.owners
        self.part = self.hidden // self.ranks
        self.block = min(self.total, 256)


def ctx_all(value):
    pieces = {0: value}
    bit = lax.axis_size("ctx") // 2
    while bit:
        for k in list(pieces):
            pieces[k | bit] = swap(pieces[k], "ctx", bit)
        bit //= 2
    return [pieces[k] for k in sorted(pieces)]


def ctx_sum(odd, even):
    bit = 1
    ranks = lax.axis_size("ctx")
    while True:
        got = swap(odd, "ctx", bit)
        bit *= 2
        if bit == ranks:
            return even, got
        total = even + got.astype(F32)
        even = total[0::2]
        odd = total[1::2].astype(BF16)


def fsdp_all(value):
    size = lax.axis_size("fsdp")
    pieces = [None] * size
    for k in range(0, size, 2):
        pieces[k] = value if k == 0 else swap(value, "fsdp", k)
    for k in range(0, size, 2):
        pieces[k + 1] = swap(pieces[k], "fsdp", 1)
    return pieces


def fsdp_sum(odd, even):
    got = swap(odd, "fsdp", 1)
    total = even[0] + got[0].astype(F32)
    terms = []
    for i in range(1, even.shape[0]):
        pair = (even[i] + got[i].astype(F32)).astype(BF16)
        terms.append(swap(pair, "fsdp", 2 * i))
    for term in terms:
        total = total + term.astype(F32)
    return total.astype(BF16)


def rows_of(rank, length):
    return pl.ds(pl.multiple_of(rank * length, length), length)


def normalise(value):
    scale = lax.rsqrt(jnp.mean(value * value, -1, keepdims=True) + EPS)
    return value * scale, scale


def turn(value, cosine, sine):
    width = value.shape[1]
    lane = lax.broadcasted_iota(jnp.int32, value.shape, 1)
    other = jnp.where(
        lane % HD < HD // 2,
        pltpu.roll(value, width - HD // 2, 1),
        pltpu.roll(value, HD // 2, 1),
    )
    return value * cosine + other * sine


def causal(start, rows, keys):
    at = start + lax.broadcasted_iota(jnp.int32, (rows, keys), 0)
    return at >= lax.broadcasted_iota(jnp.int32, (rows, keys), 1)


def kv_slot(plan, rank, head):
    first = lax.div(rank * plan.heads, plan.group)
    return lax.div(rank * plan.heads + head, plan.group) - first


def forward_attention(plan):
    n, f, r, t, length = plan.ranks, plan.owners, plan.rows, plan.total, plan.length
    scale = HD ** (-0.5)

    def kernel(ids, *refs):
        xs, packs = refs[:n], refs[n : n + f]
        cosine, sine = refs[n + f], refs[n + f + 1]
        h_out, qkv_out, lse_out, o_out, g_out = refs[n + f + 2 : n + f + 7]
        o_parts = refs[n + f + 7 : n + f + 7 + n]
        w_s, g_s, k_s, v_s = refs[n + f + 7 + n :]
        owner, rank = ids[0], ids[1]
        low = plan.pack_rows - 16
        for k in range(f):
            w_s[owner ^ k] = packs[k][:, : plan.qkv_cols]
            tail = packs[k][low:, :LANES].astype(F32)
            g_s[owner ^ k] = tail
        for j in range(f):
            g_out[0:2, j * r : (j + 1) * r] = g_s[j, r - low : r - low + 2, :r]
        gain = g_out[0:1, :]
        for j in range(n):
            z, _ = normalise(xs[j][...].astype(F32))
            h_out[rows_of(rank ^ j, length), :] = (z * gain).astype(BF16)
        total = None
        for j in range(f):
            term = dot(h_out[:, j * r : (j + 1) * r], w_s[j, :r, :])
            total = term if total is None else total + term
        qkv_out[...] = turn(total, cosine[...], sine[...]).astype(BF16)
        for s in range(plan.kv):
            at = plan.q_cols + s * HD
            k_s[s] = qkv_out[:, at : at + HD]
            at += plan.kv_cols
            v_s[s] = qkv_out[:, at : at + HD]
        for head in range(plan.heads):
            slot = kv_slot(plan, rank, head)
            for start in range(0, t, plan.block):
                end = start + plan.block
                q = qkv_out[start:end, head * HD : (head + 1) * HD]
                scores = dot(q, k_s[slot, :end, :], COLS) * scale
                scores = jnp.where(causal(start, plan.block, end), scores, -1e30)
                top = jnp.max(scores, -1, keepdims=True)
                probs = jnp.exp(scores - top)
                total = jnp.sum(probs, -1, keepdims=True)
                mixed = dot(probs.astype(BF16), v_s[slot, :end, :]) / total
                o_out[start:end, head * HD : (head + 1) * HD] = mixed.astype(BF16)
                lse_out[start:end, head : head + 1] = top + jnp.log(total)
        for j in range(n):
            o_parts[j][...] = o_out[rows_of(rank ^ j, length), :]

    outs = [
        shape((t, plan.width), BF16),
        shape((t, plan.qkv_cols), BF16),
        shape((t, LANES), F32),
        shape((t, plan.q_cols), BF16),
        shape((8, plan.width), F32),
    ] + [shape((length, plan.q_cols), BF16)] * n
    scratch = [
        ((f, plan.pack_rows, plan.qkv_cols), BF16),
        ((f, 16, LANES), F32),
        ((plan.kv, t, HD), BF16),
        ((plan.kv, t, HD), BF16),
    ]
    return kernel, outs, scratch


def out_projection(plan):
    n, f, r, length, o = plan.ranks, plan.owners, plan.rows, plan.length, plan.out_cols

    def kernel(ids, x, gains, *refs):
        parts, weights = refs[:n], refs[n : 2 * n]
        y_out, h_out, a_out, a_s, b_s, y_s, wide = refs[2 * n :]
        owner, rank = ids[0], ids[1]
        for j in range(n):
            a_s[rank ^ j] = parts[j][...]
        for j in range(n):
            wide[:, j * plan.q_cols : (j + 1) * plan.q_cols] = a_s[j]
        a_out[...] = wide[:, : plan.width]
        for j in range(f):
            b_s[j] = a_out[:, j * r : (j + 1) * r]
        for j in range(n):
            total = None
            for k in range(f):
                term = dot(b_s[owner ^ k], weights[j][k, :r, :])
                total = term if total is None else total + term
            y_s[rank ^ j] = total
        for j in range(n):
            at = slice(j * o, (j + 1) * o)
            y_out[:, at] = x[:, at].astype(F32) + y_s[j, :, :o]
        z, _ = normalise(y_out[...])
        h_out[...] = (z * gains[1:2, :]).astype(BF16)

    outs = [
        shape((length, plan.width), F32),
        shape((length, plan.width), BF16),
        shape((length, plan.width), BF16),
    ]
    scratch = [
        ((n, length, plan.q_cols), BF16),
        ((f, length, r), BF16),
        ((n, length, plan.out_pad), F32),
        ((length, n * plan.q_cols), BF16),
    ]
    return kernel, outs, scratch


def parts_out(total, odd, even, rank, ranks, length):
    for i in range(ranks // 2):
        even[i] = total[rows_of(rank ^ (2 * i), length), :]
        odd[i] = total[rows_of(rank ^ (2 * i + 1), length), :].astype(BF16)


def sum_shapes(dims):
    return [shape(dims, BF16), shape(dims, F32)]


def feed_forward(plan):
    n, f, r, t, length = plan.ranks, plan.owners, plan.rows, plan.total, plan.length
    pr = plan.part_rows

    def kernel(ids, *refs):
        hs, cs = refs[:n], refs[n : 2 * n]
        gus, downs = refs[2 * n : 2 * n + f], refs[2 * n + f : 2 * n + 2 * f]
        refs = refs[2 * n + 2 * f :]
        h_out, c_out, w_out, act_out, dg_out, du_out, odd, even, gu_s, d_s, acc = refs
        owner, rank = ids[0], ids[1]
        for j in range(n):
            at = rows_of(rank ^ j, length)
            h_out[at, :] = hs[j][...]
            c_out[at, :] = cs[j][...]
        for k in range(f):
            gu_s[owner ^ k] = gus[k][...]
            d_s[owner ^ k] = downs[k][...]
        for j in range(f):
            w_out[j * pr : (j + 1) * pr, :] = d_s[j]
        gate = upper = None
        for j in range(f):
            h = h_out[:, j * r : (j + 1) * r]
            one = dot(h, gu_s[j, 0])
            two = dot(h, gu_s[j, 1])
            gate = one if gate is None else gate + one
            upper = two if upper is None else upper + two
        d_act = dot(c_out[...], w_out[...], COLS)
        sigma = jax.nn.sigmoid(gate)
        act_out[...] = (gate * sigma * upper).astype(BF16)
        dg_out[...] = (d_act * upper * sigma * (1.0 + gate * (1.0 - sigma))).astype(BF16)
        du_out[...] = (d_act * gate * sigma).astype(BF16)
        for j in range(f):
            acc[:, j * r : (j + 1) * r] = dot(dg_out[...], gu_s[j, 0], COLS) + dot(
                du_out[...], gu_s[j, 1], COLS
            )
        parts_out(acc, odd, even, rank, n, length)

    outs = [
        shape((t, plan.width), BF16),
        shape((t, plan.width), BF16),
        shape((plan.part, plan.width), BF16),
        shape((t, plan.part), BF16),
        shape((t, plan.part), BF16),
        shape((t, plan.part), BF16),
    ] + sum_shapes((n // 2, length, plan.width))
    scratch = [
        ((f, 2, r, plan.part), BF16),
        ((f, pr, plan.width), BF16),
        ((t, plan.width), F32),
    ]
    return kernel, outs, scratch


def feed_forward_grads(plan):
    n, f, r, length, pr = plan.ranks, plan.owners, plan.rows, plan.length, plan.part_rows

    def kernel(ids, h, c, w, act, dg, du, *refs):
        g_odd, g_even, u_odd, u_even, d_odd, d_even, odd, even, g_s, u_s, d_s, acc = refs
        owner, rank = ids[0], ids[1]
        for j in range(f):
            block = h[:, j * r : (j + 1) * r]
            g_s[j] = dot(block, dg[...], ROWS)
            u_s[j] = dot(block, du[...], ROWS)
            d_s[j] = dot(act[:, j * pr : (j + 1) * pr], c[...], ROWS)
        for i in range(f // 2):
            for src, o_ref, e_ref in (
                (g_s, g_odd, g_even),
                (u_s, u_odd, u_even),
                (d_s, d_odd, d_even),
            ):
                e_ref[i] = src[owner ^ (2 * i)]
                o_ref[i] = src[owner ^ (2 * i + 1)].astype(BF16)
        acc[...] = dot(act[...], w[...])
        parts_out(acc, odd, even, rank, n, length)

    gu = (f // 2, r, plan.part)
    down = (f // 2, pr, plan.width)
    outs = (
        sum_shapes(gu)
        + sum_shapes(gu)
        + sum_shapes(down)
        + sum_shapes((n // 2, length, plan.width))
    )
    scratch = [
        ((f, r, plan.part), F32),
        ((f, r, plan.part), F32),
        ((f, pr, plan.width), F32),
        ((plan.total, plan.width), F32),
    ]
    return kernel, outs, scratch


def residual_backward(plan):
    n, f, r, length, o = plan.ranks, plan.owners, plan.rows, plan.length, plan.out_cols

    def kernel(ids, keep, got, y, cot, gains, *refs):
        weights = refs[:n]
        dy_out, dyb_out, g_out = refs[n : n + 3]
        parts = refs[n + 3 : 2 * n + 3]
        c_s, b_s, wide, p_s = refs[2 * n + 3 :]
        owner, rank = ids[0], ids[1]
        d_h = keep[0] + got[0].astype(F32)
        z, scale = normalise(y[...])
        g_out[0:1, :] = jnp.sum(d_h * z, 0, keepdims=True)
        d_z = d_h * gains[1:2, :]
        d_y = cot[...].astype(F32) + scale * (d_z - z * jnp.mean(d_z * z, -1, keepdims=True))
        dy_out[...] = d_y
        dyb_out[...] = d_y.astype(BF16)
        for j in range(n):
            c_s[j] = dyb_out[:, j * o : (j + 1) * o]
        for k in range(f):
            total = None
            for j in range(n):
                term = dot(c_s[rank ^ j], weights[j][k, :r, :o], COLS)
                total = term if total is None else total + term
            b_s[owner ^ k] = total.astype(BF16)
        wide[...] = jnp.zeros_like(wide)
        for j in range(f):
            wide[:, j * r : (j + 1) * r] = b_s[j]
        for j in range(n):
            p_s[j] = wide[:, j * plan.q_cols : (j + 1) * plan.q_cols]
        for j in range(n):
            parts[j][...] = p_s[rank ^ j]

    outs = [
        shape((length, plan.width), F32),
        shape((length, plan.width), BF16),
        shape((8, plan.width), F32),
    ] + [shape((length, plan.q_cols), BF16)] * n
    scratch = [
        ((n, length, o), BF16),
        ((f, length, r), BF16),
        ((length, n * plan.q_cols), BF16),
        ((n, length, plan.q_cols), BF16),
    ]
    return kernel, outs, scratch


def out_grads(plan):
    n, f, r, length, o = plan.ranks, plan.owners, plan.rows, plan.length, plan.out_cols

    def kernel(ids, attn, dyb, odd, even, b_s, c_s):
        owner, rank = ids[0], ids[1]
        for j in range(f):
            b_s[j] = attn[:, j * r : (j + 1) * r]
        for j in range(n):
            c_s[j] = dyb[:, j * o : (j + 1) * o]
        for i in range(n // 2):
            for k in range(f):
                block = b_s[owner ^ k]
                even[i, k] = dot(block, c_s[rank ^ (2 * i)], ROWS)
                odd[i, k] = dot(block, c_s[rank ^ (2 * i + 1)], ROWS).astype(BF16)

    outs = sum_shapes((n // 2, f, r, o))
    scratch = [((f, length, r), BF16), ((n, length, o), BF16)]
    return kernel, outs, scratch


def backward_attention(plan):
    n, f, r, t, length = plan.ranks, plan.owners, plan.rows, plan.total, plan.length
    scale = HD ** (-0.5)

    def kernel(ids, qkv, lse, mixed, cosine, sine, *refs):
        parts, xs, packs = refs[:n], refs[n : 2 * n], refs[2 * n : 2 * n + f]
        refs = refs[2 * n + f :]
        d_out, odd, even, g_out, w_s, k_s, v_s, d_s, dk_s, dv_s, acc, raw = refs
        owner, rank = ids[0], ids[1]
        for k in range(f):
            w_s[owner ^ k] = packs[k][:, : plan.qkv_cols]
        for j in range(n):
            d_s[rows_of(rank ^ j, length), :] = parts[j][...]
        for s in range(plan.kv):
            at = plan.q_cols + s * HD
            k_s[s] = qkv[:, at : at + HD]
            at += plan.kv_cols
            v_s[s] = qkv[:, at : at + HD]
        dk_s[...] = jnp.zeros_like(dk_s)
        dv_s[...] = jnp.zeros_like(dv_s)
        if plan.used < plan.qkv_cols:
            raw[:, plan.used :] = jnp.zeros((t, plan.qkv_cols - plan.used), F32)
        for head in range(plan.heads):
            cols = slice(head * HD, (head + 1) * HD)
            slot = kv_slot(plan, rank, head)
            for start in range(0, t, plan.block):
                end = start + plan.block
                q = qkv[start:end, cols]
                d_o = d_s[start:end, cols]
                keys = k_s[slot, :end, :]
                delta = jnp.sum(
                    d_o.astype(F32) * mixed[start:end, cols].astype(F32), -1, keepdims=True
                )
                scores = dot(q, keys, COLS) * scale
                probs = jnp.where(
                    causal(start, plan.block, end),
                    jnp.exp(scores - lse[start:end, head : head + 1]),
                    0.0,
                )
                dv_s[slot, :end, :] += dot(probs.astype(BF16), d_o, ROWS)
                d_p = dot(d_o, v_s[slot, :end, :], COLS)
                d_sc = (probs * (d_p - delta)).astype(BF16)
                raw[start:end, cols] = dot(d_sc, keys) * scale
                dk_s[slot, :end, :] += dot(d_sc, q, ROWS) * scale
        for s in range(plan.kv):
            at = plan.q_cols + s * HD
            raw[:, at : at + HD] = dk_s[s]
            at += plan.kv_cols
            raw[:, at : at + HD] = dv_s[s]
        d_out[...] = turn(raw[...], cosine[...], -sine[...]).astype(BF16)
        for j in range(f):
            acc[:, j * r : (j + 1) * r] = dot(d_out[...], w_s[j, :r, :], COLS)
        gain = None
        for j in range(n):
            z, _ = normalise(xs[j][...].astype(F32))
            term = jnp.sum(acc[rows_of(rank ^ j, length), :] * z, 0, keepdims=True)
            gain = term if gain is None else gain + term
        g_out[0:1, :] = gain
        parts_out(acc, odd, even, rank, n, length)

    outs = (
        [shape((t, plan.qkv_cols), BF16)]
        + sum_shapes((n // 2, length, plan.width))
        + [shape((8, plan.width), F32)]
    )
    scratch = [
        ((f, plan.pack_rows, plan.qkv_cols), BF16),
        ((plan.kv, t, HD), BF16),
        ((plan.kv, t, HD), BF16),
        ((t, plan.q_cols), BF16),
        ((plan.kv, t, HD), F32),
        ((plan.kv, t, HD), F32),
        ((t, plan.width), F32),
        ((t, plan.qkv_cols), F32),
    ]
    return kernel, outs, scratch


def pack_grads(plan):
    f, r, o = plan.owners, plan.rows, plan.out_cols

    def kernel(ids, h, d_qkv, gain_one, gain_two, keep, got, odd, even, p_s):
        owner = ids[0]
        p_s[...] = jnp.zeros_like(p_s)
        for j in range(f):
            p_s[j, :r, : plan.qkv_cols] = dot(h[:, j * r : (j + 1) * r], d_qkv[...], ROWS)
            p_s[j, r : r + 1, :r] = gain_one[0:1, j * r : (j + 1) * r]
            p_s[j, r + 1 : r + 2, :r] = gain_two[0:1, j * r : (j + 1) * r]
        for k in range(f):
            at = slice(plan.qkv_cols, plan.qkv_cols + o)
            p_s[owner ^ k, :r, at] = keep[0, k] + got[0, k].astype(F32)
        for i in range(f // 2):
            even[i] = p_s[owner ^ (2 * i)]
            odd[i] = p_s[owner ^ (2 * i + 1)].astype(BF16)

    outs = sum_shapes((f // 2, plan.pack_rows, plan.pack_cols))
    scratch = [((f, plan.pack_rows, plan.pack_cols), F32)]
    return kernel, outs, scratch


def input_backward(plan):
    def kernel(ids, keep, got, d_y, x, gains, out):
        d_h = keep[0] + got[0].astype(F32)
        z, scale = normalise(x[...].astype(F32))
        d_z = d_h * gains[0:1, :]
        out[...] = d_y[...] + scale * (d_z - z * jnp.mean(d_z * z, -1, keepdims=True))

    return kernel, shape((plan.length, plan.width), F32), []


def spread_hidden(plan):
    n, f, r, pr = plan.ranks, plan.owners, plan.rows, plan.part_rows

    def kernel(ids, *refs):
        gates, uppers, downs = refs[:n], refs[n : 2 * n], refs[2 * n : 3 * n]
        gu_out, d_out, g_s, u_s, d_s = refs[3 * n :]
        rank = ids[1]
        for j in range(n):
            g_s[rank ^ j] = gates[j][...].astype(F32)
            u_s[rank ^ j] = uppers[j][...].astype(F32)
            d_s[rank ^ j] = downs[j][...].astype(F32)
        for j in range(n):
            d_out[j * pr : (j + 1) * pr, :] = d_s[j]
            for k in range(f):
                src = slice(k * pr, (k + 1) * pr)
                at = k * n * pr + j * pr
                gu_out[0, :, at : at + pr] = g_s[j, :, src]
                gu_out[1, :, at : at + pr] = u_s[j, :, src]

    outs = [shape((2, r, plan.hidden), F32), shape((n * pr, plan.width), F32)]
    scratch = [((n, r, plan.part), F32), ((n, r, plan.part), F32), ((n, pr, plan.width), F32)]
    return kernel, outs, scratch


def spread_pack(plan):
    n, r, o = plan.ranks, plan.rows, plan.out_cols

    def kernel(ids, *refs):
        packs = refs[:n]
        qkv_out, out_out, g_out, p_s = refs[n:]
        rank = ids[1]
        for j in range(n):
            p_s[rank ^ j] = packs[j][...].astype(F32)
        gain = None
        for j in range(n):
            count = min(plan.heads, H - j * plan.heads) * HD
            if count > 0:
                at = j * plan.q_cols
                qkv_out[:, at : at + count] = p_s[j, :r, :count]
            at = plan.qkv_cols
            out_out[:, j * o : (j + 1) * o] = p_s[j, :r, at : at + o]
            term = p_s[j, r : r + 2, :r]
            gain = term if gain is None else gain + term
        g_out[0:2, :] = gain
        for kind in range(2):
            for head in range(KVH):
                total = None
                for j in range(n):
                    slot = head - plan.kv_first[j]
                    if 0 <= slot < plan.kv:
                        at = plan.q_cols + kind * plan.kv_cols + slot * HD
                        term = p_s[j, :r, at : at + HD]
                        total = term if total is None else total + term
                at = (H + kind * KVH + head) * HD
                qkv_out[:, at : at + HD] = total

    outs = [
        shape((r, (H + 2 * KVH) * HD), F32),
        shape((r, plan.width), F32),
        shape((8, r), F32),
    ]
    scratch = [((n, plan.pack_rows, plan.pack_cols), F32)]
    return kernel, outs, scratch


def body(tokens, gain_attn, w_qkv, w_out, gain_ffn, w_gate_up, w_down, cotangent):
    plan = Plan(tokens, w_qkv, w_down)
    rank = lax.axis_index("ctx")
    owner = lax.axis_index("fsdp")
    ids = jnp.stack([owner, rank]).astype(jnp.int32)
    ranks, rows = plan.ranks, plan.rows
    kv_base = (rank * plan.heads) // plan.group
    x_loc = tokens[0]
    cot_loc = cotangent[0]

    def call(maker, *args):
        kernel, outs, scratch = maker(plan)
        return run(kernel, maker.__name__, outs, ids, args, scratch)

    q_end = H * HD
    k_end = (H + KVH) * HD
    kv_room = ((0, 0), (0, (plan.kv_pad - KVH) * HD))
    q_room = jnp.pad(w_qkv[:, :q_end], ((0, 0), (0, (ranks * plan.heads - H) * HD)))
    k_room = jnp.pad(w_qkv[:, q_end:k_end], kv_room)
    v_room = jnp.pad(w_qkv[:, k_end:], kv_room)
    slices = [
        lax.dynamic_slice_in_dim(q_room, rank * plan.q_cols, plan.q_cols, 1),
        lax.dynamic_slice_in_dim(k_room, kv_base * HD, plan.kv_cols, 1),
        lax.dynamic_slice_in_dim(v_room, kv_base * HD, plan.kv_cols, 1),
        jnp.zeros((rows, plan.qkv_cols - plan.used), BF16),
        lax.dynamic_slice_in_dim(w_out, rank * plan.out_cols, plan.out_cols, 1),
        jnp.zeros((rows, plan.out_pad - plan.out_cols), BF16),
    ]
    gains = jnp.pad(
        jnp.stack([gain_attn, gain_ffn]),
        ((0, plan.pack_rows - rows - 2), (0, plan.pack_cols - rows)),
    )
    pack = jnp.concatenate([jnp.concatenate(slices, 1), gains], 0)
    column = jnp.arange(plan.part, dtype=jnp.int32)
    source = (
        (column // plan.part_rows) * w_down.shape[0]
        + rank * plan.part_rows
        + column % plan.part_rows
    )
    chooser = (jnp.arange(plan.hidden, dtype=jnp.int32)[:, None] == source[None, :]).astype(BF16)
    gu_part = dot(w_gate_up.reshape(2 * rows, plan.hidden), chooser).astype(BF16)
    gu_part = gu_part.reshape(2, rows, plan.part)
    down_part = lax.dynamic_slice_in_dim(w_down, rank * plan.part_rows, plan.part_rows, 0)

    lane = jnp.arange(plan.qkv_cols, dtype=jnp.int32)
    half = HD // 2
    freqs = jnp.exp(-jnp.log(10000.0) * (lane % half).astype(F32) / half)
    angles = jnp.arange(plan.total, dtype=jnp.int32).astype(F32)[:, None] * freqs[None, :]
    turned = lane < plan.q_cols + plan.kv_cols
    cosine = jnp.where(turned, jnp.cos(angles), 1.0)
    sine = jnp.where(turned, jnp.sin(angles), 0.0) * jnp.where(lane % HD < half, -1.0, 1.0)

    packs = fsdp_all(pack)
    x_all = ctx_all(x_loc)
    out_own = jnp.stack([piece[:, plan.qkv_cols :] for piece in packs])
    out_all = ctx_all(out_own)
    cot_all = ctx_all(cot_loc)
    gus = fsdp_all(gu_part)
    downs = fsdp_all(down_part)

    fwd = call(forward_attention, *x_all, *packs, cosine, sine)
    h_one, qkv, lse, mixed, gain_rows = fwd[:5]
    o_parts = fwd[5:]
    got = [o_parts[0]] + [swap(o_parts[k], "ctx", k) for k in range(1, ranks)]
    resid, h_two_loc, attn = call(out_projection, x_loc, gain_rows, *got, *out_all)
    h_two_all = ctx_all(h_two_loc)
    ffn = call(feed_forward, *h_two_all, *cot_all, *gus, *downs)
    h_two, cots, down_full, act, d_gate, d_upper, odd, even = ffn
    keep, came = ctx_sum(odd, even)
    grads = call(feed_forward_grads, h_two, cots, down_full, act, d_gate, d_upper)
    back = call(residual_backward, keep, came, resid, cot_loc, gain_rows, *out_all)
    d_resid, d_resid_b, gain_two = back[:3]
    d_parts = back[3:]
    d_got = [d_parts[0]] + [swap(d_parts[k], "ctx", k) for k in range(1, ranks)]
    o_odd, o_even = call(out_grads, attn, d_resid_b)
    o_keep, o_came = ctx_sum(o_odd, o_even)
    d_qkv, odd, even, gain_one = call(
        backward_attention, qkv, lse, mixed, cosine, sine, *d_got, *x_all, *packs
    )
    keep, came = ctx_sum(odd, even)
    p_odd, p_even = call(pack_grads, h_one, d_qkv, gain_one, gain_two, o_keep, o_came)
    d_input = call(input_backward, keep, came, d_resid, x_loc, gain_rows)

    gate_own = fsdp_sum(grads[0], grads[1])
    upper_own = fsdp_sum(grads[2], grads[3])
    down_own = fsdp_sum(grads[4], grads[5])
    keep, came = ctx_sum(grads[6], grads[7])
    result = (resid + keep[0] + came[0].astype(F32)).astype(BF16)
    gu_out, down_out = call(
        spread_hidden, *ctx_all(gate_own), *ctx_all(upper_own), *ctx_all(down_own)
    )
    pack_own = fsdp_sum(p_odd, p_even)
    qkv_out, out_out, gain_out = call(spread_pack, *ctx_all(pack_own))
    return (
        result[None],
        d_input[None],
        gain_out[0],
        qkv_out,
        out_out,
        gain_out[1],
        gu_out,
        down_out,
    )


def solution(mesh):
    in_specs = (
        P("fsdp", "ctx", None),
        P("fsdp"),
        P("fsdp", None),
        P("fsdp", None),
        P("fsdp"),
        P(None, "fsdp", None),
        P("fsdp", None),
        P("fsdp", "ctx", None),
    )
    out_specs = (
        P("fsdp", "ctx", None),
        P("fsdp", "ctx", None),
        P("fsdp"),
        P("fsdp", None),
        P("fsdp", None),
        P("fsdp"),
        P(None, "fsdp", None),
        P("fsdp", None),
    )
    return jax.shard_map(body, mesh=mesh, in_specs=in_specs, out_specs=out_specs, check_vma=False)
```
